32 devices in a mesh: dp: 2 (over core), row: 4 (over y, x), col: 4 (over z).
Axes of the slice: x: 2, y: 2, z: 4, core: 2. Of those that a mesh axis runs over, the one named last changes fastest.
Arguments:
- tokens: bfloat16 [256, 8192], P(('dp', 'col'), 'row'), may hold values from -6 to 6
- cotangent: bfloat16 [256, 8192], P(('dp', 'col'), 'row'), may hold values from -6 to 6
- weight: bfloat16 [8192, 16384], P('row', 'col'), may hold values from -0.125 to 0.125
- block_mask: int32 [32, 64], P('row', 'col'), may hold values 0 or 1
Outputs:
- output: bfloat16 [256, 8192], P(('dp', 'col'), 'row')
- input_grad: bfloat16 [256, 8192], P(('dp', 'col'), 'row')
- weight_grad: float32 [8192, 2, 8192], P('row', 'dp', 'col')
The draws below stay inside these ranges and needn't reach their ends.
Inputs may be any that keep to these rules, and one draw needn't show every extreme that they name: block_mask holds only 0 and 1.
All inputs are finite; a program needn't handle non-finite values. No bound on the sum of `block_mask` on one device may be relied on, other than what follows from the above.
Results may differ from the reference program's by a relative error of at most 0.0032.
Values may be sent and summed in bfloat16 or wider, within the bound.
A program may use at most 128 MiB of HBM per device.

```python
import math
import jax
import jax.numpy as jnp

D = 8192
F = 16384
BLOCK = 256
TOKENS = 256
N_DP = 2
N_COL = 4


def set_ends(result, key, smallest, high):
    longest = result.shape.index(max(result.shape))
    spots = []
    for shift in (0, 1):
        where = [jax.random.randint(jax.random.fold_in(key, axis), (), 0, length) for axis, length in enumerate(result.shape)]
        where[longest] = (where[longest] + shift) % result.shape[longest]
        spots.append(tuple(where))
    return result.at[spots[0]].set(smallest).at[spots[1]].set(high)


def block_levels(key, extent, split, least, top_value):
    def one(axis_at, parts):
        draws = jax.random.uniform(jax.random.fold_in(jax.random.fold_in(key, 6), axis_at), (parts,), jnp.float32, least / len(split), top_value / len(split))
        return jnp.repeat(jnp.exp(draws), extent[axis_at] // parts).reshape((-1,) + (1,) * (len(extent) - axis_at - 1))

    level = one(*split[0])
    for cut in split[1:]:
        level = level * one(*cut)
    return level


def normal_values(stream_key, shape, width, bound, split=(), kind=jnp.bfloat16):
    result = width * jax.random.normal(stream_key, shape, jnp.float32)
    if split:
        result = result * block_levels(stream_key, shape, split, -0.22, 0.18)
    return jnp.clip(result, -bound, bound).astype(kind)


def setup_inputs(seed: int = 0) -> dict:
    seeds = jax.random.split(jax.random.key(seed), 5)
    tokens = normal_values(seeds[0], (TOKENS, D), 1.0, 6.0, ((0, 8), (1, 4)))
    cotangent = normal_values(seeds[1], (TOKENS, D), 1.0, 6.0, ((0, 8), (1, 4)))
    weight = normal_values(seeds[2], (D, F), (D // 4) ** -0.5, 0.125, ((0, 4), (1, 4)))
    block_mask = set_ends((jax.random.randint(seeds[3], (D // BLOCK, F // BLOCK), 0, 4) < 1).astype(jnp.int32), jax.random.fold_in(seeds[3], 1), 0, 1)
    return dict(tokens=tokens, cotangent=cotangent, weight=weight, block_mask=block_mask)


def expand_mask(block_mask):
    kept_blocks = block_mask.astype(jnp.bfloat16)
    return jnp.repeat(jnp.repeat(kept_blocks, BLOCK, axis=0), BLOCK, axis=1)

def reference(tokens, cotangent, weight, block_mask):
    kept = expand_mask(block_mask)
    masked = weight * kept
    pre = jnp.dot(tokens, masked, preferred_element_type=jnp.float32)
    hidden = jax.nn.silu(pre).astype(jnp.bfloat16)
    projected = jnp.dot(hidden, masked.T, preferred_element_type=jnp.float32)
    output = (tokens.astype(jnp.float32) + projected).astype(jnp.bfloat16)
    grad_hidden = jnp.dot(cotangent, masked, preferred_element_type=jnp.float32)
    sigmoid_pre = jax.nn.sigmoid(pre)
    grad_pre = (grad_hidden * sigmoid_pre * (1.0 + pre * (1.0 - sigmoid_pre))).astype(jnp.bfloat16)
    back = jnp.dot(grad_pre, masked.T, preferred_element_type=jnp.float32)
    input_grad = (cotangent.astype(jnp.float32) + back).astype(jnp.bfloat16)
    full = jnp.dot(cotangent.T, hidden, preferred_element_type=jnp.float32)
    full = full + jnp.dot(tokens.T, grad_pre, preferred_element_type=jnp.float32)
    full = full * kept.astype(jnp.float32) * (1.0 / math.sqrt(TOKENS))
    share_cols = F // (N_COL * N_DP)
    weight_grad = full.reshape(D, N_COL, N_DP, share_cols).transpose(0, 2, 1, 3).reshape(D, N_DP, N_COL * share_cols)
    return (output, input_grad, weight_grad)
```

```python
import functools
import math

import jax
import jax.numpy as jnp
from jax import lax
from jax.experimental import pallas as pl
from jax.experimental.pallas import tpu as pltpu
from jax.sharding import PartitionSpec as P

BLOCK = 256
RS1_TYPE = jnp.bfloat16
RS2_TYPE = jnp.bfloat16
PAIR_TYPE = jnp.float32
COL_TYPE = jnp.bfloat16


def flip1(i):
    return i + 1 - 2 * (i % 2)


def flip2(i):
    return (i + 2) % 4


def flip(i, bits):
    if bits == 0:
        return i
    if bits == 1:
        return flip1(i)
    if bits == 2:
        return flip2(i)
    return 3 - i


def ffn_kernel(tok_hbm, cot_hbm, w_hbm, mask_ref, out_ref, ig_ref, x_out, h_out,
               x_buf, w_buf, keep, s1, r1, s2, r2, h_buf, o_own, pair_s, pair_r, z_s, z_r,
               local_sem, w_sem, send_sem, recv_sem):
    d = lax.axis_index("dp")
    r = lax.axis_index("row")
    c = lax.axis_index("col")
    tok_n = tok_hbm.shape[0]
    quarter = w_buf.shape[2]
    share = 4 * quarter
    half = x_buf.shape[2]
    feats = w_buf.shape[1]
    other = (1 - d, r, c)
    row_peer = {a: (d, flip(r, a), c) for a in (1, 2)}
    col_peer = {a: (d, r, flip(c, a)) for a in (1, 2, 3)}

    tok_cp = pltpu.make_async_copy(tok_hbm, x_buf.at[0, d, pl.ds(0, tok_n)], local_sem.at[0])
    cot_cp = pltpu.make_async_copy(cot_hbm, x_buf.at[0, d, pl.ds(tok_n, tok_n)], local_sem.at[1])
    tok_cp.start()
    cot_cp.start()
    w_cps = []
    for t in (3, 1, 2, 0):
        q = flip(r, t)
        cols = pl.ds(pl.multiple_of(d * share + q * quarter, 128), quarter)
        cp = pltpu.make_async_copy(w_hbm.at[:, cols], w_buf.at[q], w_sem.at[t])
        cp.start()
        w_cps.append((q, cp))

    barrier = pltpu.get_barrier_semaphore()
    peers = [other] + list(row_peer.values()) + list(col_peer.values())
    for peer in peers:
        pl.semaphore_signal(barrier, inc=1, device_id=peer, device_id_type=pl.DeviceIdType.MESH)
    pl.semaphore_wait(barrier, len(peers))

    count = [0]
    msgs = {}

    def msg(name, src, dst, peer):
        i = count[0]
        count[0] += 1
        cp = pltpu.make_async_remote_copy(
            src_ref=src, dst_ref=dst, send_sem=send_sem.at[i], recv_sem=recv_sem.at[i],
            device_id=peer, device_id_type=pl.DeviceIdType.MESH)
        cp.start()
        msgs[name] = cp

    def arrive(name):
        msgs[name].wait_recv()

    tok_cp.wait()
    cot_cp.wait()
    msg(("xp", 0), x_buf.at[0, d], x_buf.at[0, d], other)
    for s in (1, 2, 3):
        msg(("xz", s), x_buf.at[0, d], x_buf.at[s, d], col_peer[s])

    for q, cp in w_cps:
        cp.wait()
        for i in range(feats // BLOCK):
            rows = pl.ds(i * BLOCK, BLOCK)
            w_buf[q, rows, :] = w_buf[q, rows, :] * mask_ref[q, pl.ds(i, 1), :].astype(jnp.bfloat16)

    def order(s):
        return (1, 2) if s % 2 == 0 else (2, 1)

    out_cps = []

    def fwd(s):
        arrive(("xz", s))
        msg(("xp", s), x_buf.at[s, d], x_buf.at[s, d], other)

    def stage_a(s):
        a, b = order(s)
        arrive(("xp", s))
        x = x_buf[s].reshape(2 * half, feats)
        cp = pltpu.make_async_copy(x_buf.at[s], x_out.at[s], local_sem.at[2 + s])
        cp.start()
        out_cps.append(cp)
        for k, t in ((1, 3), (0, a)):
            q = flip(r, t)
            s1[s, k] = jnp.dot(x, w_buf[q], preferred_element_type=jnp.float32).astype(s1.dtype)
            msg(("r1", s, k), s1.at[s, k], r1.at[s, k], row_peer[a])
        for k, t in ((1, b), (0, 0)):
            q = flip(r, t)
            keep[s, k] = jnp.dot(x, w_buf[q], preferred_element_type=jnp.float32)

    def stage_b(s):
        a, b = order(s)
        arrive(("r1", s, 1))
        s2[s] = (keep[s, 1] + r1[s, 1].astype(jnp.float32)).astype(s2.dtype)
        msg(("r2", s), s2.at[s], r2.at[s], row_peer[b])

    def stage_c(s):
        a, b = order(s)
        arrive(("r1", s, 0))
        arrive(("r2", s))
        for p in range(2):
            lo = pl.ds(p * half, tok_n)
            hi = pl.ds(p * half + tok_n, tok_n)

            def total(rows):
                return (keep[s, 0, rows, :] + r1[s, 0, rows, :].astype(jnp.float32)
                        + r2[s, rows, :].astype(jnp.float32))

            pre = total(lo)
            grad_hidden = total(hi)
            sig = jax.nn.sigmoid(pre)
            h_buf[s, r, lo, :] = (grad_hidden * sig * (1.0 + pre * (1.0 - sig))).astype(jnp.bfloat16)
            h_buf[s, r, hi, :] = (pre * sig).astype(jnp.bfloat16)
        msg(("gb", s), h_buf.at[s, r], h_buf.at[s, r], row_peer[b])
        msg(("ga", s), h_buf.at[s, r], h_buf.at[s, r], row_peer[a])

    def stage_d(s):
        a, b = order(s)
        arrive(("gb", s))
        q = flip(r, b)
        msg(("gf", s), h_buf.at[s, q], h_buf.at[s, q], row_peer[a])

    def stage_e(s):
        arrive(("ga", s))
        arrive(("gf", s))
        cp = pltpu.make_async_copy(h_buf.at[s], h_out.at[:, pl.ds(s * 2 * half, 2 * half), :], local_sem.at[6 + s])
        cp.start()
        out_cps.append(cp)
        width = quarter

        def body(f, carry):
            rows = pl.ds(pl.multiple_of(f * width, width), width)
            acc = None
            for q in range(4):
                part = lax.dot_general(h_buf[s, q], w_buf[q, rows, :], (((1,), (1,)), ((), ())),
                                       preferred_element_type=jnp.float32)
                acc = part if acc is None else acc + part
            acc = acc.reshape(2, half, width)
            low, high = acc[0], acc[1]
            mine = jnp.where(d == 0, low, high)
            theirs = jnp.where(d == 0, high, low)
            o_own[s, :, rows] = mine
            pair_s[s, :, rows] = theirs.astype(pair_s.dtype)
            return carry

        lax.fori_loop(0, feats // width, body, 0)
        msg(("pp", s), pair_s.at[s], pair_r.at[s], other)

    def stage_f(s):
        arrive(("pp", s))
        if s == 0:
            o_own[s] = o_own[s] + pair_r[s].astype(jnp.float32)
        else:
            z_s[s] = (o_own[s] + pair_r[s].astype(jnp.float32)).astype(z_s.dtype)
            msg(("zz", s), z_s.at[s], z_r.at[s], col_peer[s])

    stage_a(0)
    fwd(1)
    stage_a(1)
    stage_b(0)
    stage_c(0)
    fwd(2)
    stage_b(1)
    stage_d(0)
    stage_a(2)
    stage_c(1)
    fwd(3)
    stage_b(2)
    stage_d(1)
    stage_a(3)
    stage_e(0)
    stage_c(2)
    stage_b(3)
    stage_d(2)
    stage_e(1)
    stage_f(0)
    stage_c(3)
    stage_f(1)
    stage_d(3)
    stage_e(2)
    stage_f(2)
    stage_e(3)
    stage_f(3)

    total = o_own[0]
    for s in (1, 2, 3):
        arrive(("zz", s))
        total = total + z_r[s].astype(jnp.float32)
    base = x_buf[0, d].astype(jnp.float32)
    out_ref[...] = (base[:tok_n] + total[tok_n:]).astype(jnp.bfloat16)
    ig_ref[...] = (base[tok_n:] + total[:tok_n]).astype(jnp.bfloat16)
    for cp in out_cps:
        cp.wait()
    for cp in msgs.values():
        cp.wait_send()


def grad_kernel(scale, mask_ref, x_ref, h_ref, out_ref):
    i = pl.program_id(0)
    rows = x_ref.shape[1]
    blocks = h_ref.shape[0] * h_ref.shape[2] // BLOCK
    per = h_ref.shape[2] // BLOCK
    lanes = 128
    step = blocks * BLOCK // lanes
    for j in range(blocks):
        def put(value):
            for k in range(BLOCK // lanes):
                place = j * (BLOCK // lanes) + k
                out_ref[pl.ds(place, rows, stride=step), :] = value[:, k * lanes:(k + 1) * lanes]

        @pl.when(mask_ref[i, j] != 0)
        def _():
            h = h_ref[j // per, :, (j % per) * BLOCK:(j % per + 1) * BLOCK]
            put(lax.dot_general(x_ref[...], h, (((0,), (0,)), ((), ())),
                                preferred_element_type=jnp.float32) * scale)

        @pl.when(mask_ref[i, j] == 0)
        def _():
            put(jnp.zeros((rows, BLOCK), jnp.float32))


def fast_on_device(tokens, cotangent, weight, block_mask):
    tok_n, feats = tokens.shape
    share = weight.shape[1] // lax.axis_size("dp")
    quarter = share // 4
    half = 2 * tok_n
    d = lax.axis_index("dp")
    tok_total = tok_n * lax.axis_size("col") * lax.axis_size("dp")
    share_mask = lax.dynamic_slice_in_dim(block_mask, d * (share // BLOCK), share // BLOCK, 1)
    wide = jnp.repeat(share_mask.astype(jnp.float32), BLOCK, axis=1)
    wide = wide.reshape(feats // BLOCK, 4, quarter).transpose(1, 0, 2)
    bf, f32 = jnp.bfloat16, jnp.float32
    vmem = pl.BlockSpec(memory_space=pltpu.VMEM)
    hbm = pl.BlockSpec(memory_space=pl.ANY)
    n_msg = 38
    out, ig, x_all, h_all = pl.pallas_call(
        ffn_kernel,
        out_shape=(
            jax.ShapeDtypeStruct((tok_n, feats), bf),
            jax.ShapeDtypeStruct((tok_n, feats), bf),
            jax.ShapeDtypeStruct((4, 2, half, feats), bf),
            jax.ShapeDtypeStruct((4, 8 * half, quarter), bf),
        ),
        in_specs=[hbm, hbm, hbm, vmem],
        out_specs=(vmem, vmem, hbm, hbm),
        scratch_shapes=[
            pltpu.VMEM((4, 2, half, feats), bf),
            pltpu.VMEM((4, feats, quarter), bf),
            pltpu.VMEM((4, 2, 2 * half, quarter), f32),
            pltpu.VMEM((4, 2, 2 * half, quarter), RS1_TYPE),
            pltpu.VMEM((4, 2, 2 * half, quarter), RS1_TYPE),
            pltpu.VMEM((4, 2 * half, quarter), RS2_TYPE),
            pltpu.VMEM((4, 2 * half, quarter), RS2_TYPE),
            pltpu.VMEM((4, 4, 2 * half, quarter), bf),
            pltpu.VMEM((4, half, feats), f32),
            pltpu.VMEM((4, half, feats), PAIR_TYPE),
            pltpu.VMEM((4, half, feats), PAIR_TYPE),
            pltpu.VMEM((4, half, feats), COL_TYPE),
            pltpu.VMEM((4, half, feats), COL_TYPE),
            pltpu.SemaphoreType.DMA((10,)),
            pltpu.SemaphoreType.DMA((4,)),
            pltpu.SemaphoreType.DMA((n_msg,)),
            pltpu.SemaphoreType.DMA((n_msg,)),
        ],
        compiler_params=pltpu.CompilerParams(
            collective_id=0, has_side_effects=True, vmem_limit_bytes=60000 * 1024),
    )(tokens, cotangent, weight, wide)
    x_all = x_all.reshape(8 * half, feats)
    lines = share // 128
    flat = pl.pallas_call(
        functools.partial(grad_kernel, 1.0 / math.sqrt(tok_total)),
        grid_spec=pltpu.PrefetchScalarGridSpec(
            num_scalar_prefetch=1,
            grid=(feats // BLOCK,),
            in_specs=[
                pl.BlockSpec((8 * half, BLOCK), lambda i, m: (0, i)),
                pl.BlockSpec((4, 8 * half, quarter), lambda i, m: (0, 0, 0)),
            ],
            out_specs=pl.BlockSpec((BLOCK * lines, 128), lambda i, m: (i, 0)),
        ),
        out_shape=jax.ShapeDtypeStruct((feats * lines, 128), f32),
    )(share_mask, x_all, h_all)
    return out, ig, flat.reshape(feats, 1, share)


def partner(block, axis, stride):
    count = lax.axis_size(axis)
    route = []
    for low in range(count):
        high = low | 1 << stride
        if high != low and high < count:
            route += [(low, high), (high, low)]
    return lax.ppermute(block, axis, route)


def expand_mask(block_mask):
    kept_blocks = block_mask.astype(jnp.bfloat16)
    return jnp.repeat(jnp.repeat(kept_blocks, BLOCK, axis=0), BLOCK, axis=1)


def slope_times(grad_hidden, pre):
    sigmoid_pre = jax.nn.sigmoid(pre)
    return (grad_hidden * sigmoid_pre * (1.0 + pre * (1.0 - sigmoid_pre))).astype(jnp.bfloat16)


def times_transpose(left, masked):
    return lax.dot_general(
        left, masked, (((1,), (1,)), ((), ())), preferred_element_type=jnp.float32
    )


def on_device(tokens, cotangent, weight, block_mask):
    kept = expand_mask(block_mask)
    masked = weight * kept
    tok_count = tokens.shape[0]
    tok_rows, cot_rows = (
        lax.all_gather(tokens, "col", axis=0, tiled=True),
        lax.all_gather(cotangent, "col", axis=0, tiled=True),
    )
    pre_part = jnp.dot(tok_rows, masked, preferred_element_type=jnp.float32)
    pre = lax.psum(pre_part, "row")
    hidden = jax.nn.silu(pre).astype(jnp.bfloat16)
    grad_part = jnp.dot(cot_rows, masked, preferred_element_type=jnp.float32)
    grad_hidden = lax.psum(grad_part, "row")
    grad_pre = slope_times(grad_hidden, pre)
    projected = lax.psum_scatter(
        times_transpose(hidden, masked), "col", scatter_dimension=0, tiled=True
    )
    output = (tokens.astype(jnp.float32) + projected).astype(jnp.bfloat16)
    back = lax.psum_scatter(
        times_transpose(grad_pre, masked), "col", scatter_dimension=0, tiled=True
    )
    input_grad = (cotangent.astype(jnp.float32) + back).astype(jnp.bfloat16)
    tok_total = tok_count * lax.axis_size("col") * lax.axis_size("dp")
    norm_scale = 1.0 / math.sqrt(tok_total)
    feat_rows = masked.shape[0]
    share_cols = masked.shape[1] // lax.axis_size("dp")
    dp_index = lax.axis_index("dp")
    low_bit = dp_index % 2
    groups = lax.axis_size("dp") // 2
    row_total = hidden.shape[0]
    hid_split = hidden.reshape(row_total, groups, 2, share_cols)
    grad_split = grad_pre.reshape(row_total, groups, 2, share_cols)
    hid_class = lax.dynamic_index_in_dim(hid_split, low_bit, 2, keepdims=False)
    grad_class = lax.dynamic_index_in_dim(grad_split, low_bit, 2, keepdims=False)
    hid_other = lax.dynamic_index_in_dim(hid_split, 1 - low_bit, 2, keepdims=False)
    grad_other = lax.dynamic_index_in_dim(grad_split, 1 - low_bit, 2, keepdims=False)
    other_tok, other_cot, other_hid, other_grad = partner(
        (tok_rows, cot_rows, hid_other, grad_other), "dp", 0
    )
    pair_tok = jnp.concatenate([tok_rows, other_tok], axis=0)
    pair_cot = jnp.concatenate([cot_rows, other_cot], axis=0)
    pair_hid = jnp.concatenate([hid_class, other_hid], axis=0)
    pair_grad = jnp.concatenate([grad_class, other_grad], axis=0)
    partial_value = jnp.einsum(
        "td,tqj->qdj", pair_cot, pair_hid, preferred_element_type=jnp.float32
    )
    partial_value = partial_value + jnp.einsum(
        "td,tqj->qdj", pair_tok, pair_grad, preferred_element_type=jnp.float32
    )
    bit_count = lax.axis_size("dp").bit_length() - 1
    for bit_level in range(bit_count - 1, 0, -1):
        halves = partial_value.reshape(2, partial_value.shape[0] // 2, feat_rows, share_cols)
        my_half = dp_index // 2**bit_level % 2
        keep_part = lax.dynamic_index_in_dim(halves, my_half, 0, keepdims=False)
        send_part = lax.dynamic_index_in_dim(halves, 1 - my_half, 0, keepdims=False)
        partial_value = keep_part + partner(send_part, "dp", bit_level)
    kept_share = lax.dynamic_slice_in_dim(kept, dp_index * share_cols, share_cols, 1)
    summed = partial_value[0] * kept_share.astype(jnp.float32) * norm_scale
    weight_grad = summed.reshape(feat_rows, 1, share_cols)
    return (output, input_grad, weight_grad)


def solution(mesh):
    in_specs = (P(("dp", "col"), "row"), P(("dp", "col"), "row"), P("row", "col"), P("row", "col"))
    out_specs = (P(("dp", "col"), "row"), P(("dp", "col"), "row"), P("row", "dp", "col"))
    sizes = (mesh.shape["dp"], mesh.shape["row"], mesh.shape["col"])
    body = fast_on_device if sizes == (2, 4, 4) else on_device
    return jax.shard_map(
        body, mesh=mesh, in_specs=in_specs, out_specs=out_specs, check_vma=False
    )
```

```python
import functools
import math

import jax
import jax.numpy as jnp
from jax import lax
from jax.experimental import pallas as pl
from jax.experimental.pallas import tpu as pltpu
from jax.sharding import PartitionSpec as P

BLOCK = 256
RS1_TYPE = jnp.bfloat16
RS2_TYPE = jnp.bfloat16
PAIR_TYPE = jnp.float32
COL_TYPE = jnp.bfloat16


def flip1(i):
    return i + 1 - 2 * (i % 2)


def flip2(i):
    return (i + 2) % 4


def flip(i, bits):
    if bits == 0:
        return i
    if bits == 1:
        return flip1(i)
    if bits == 2:
        return flip2(i)
    return 3 - i


def place_of(c, j):
    side = c // 2
    near = c + side * (3 - 2 * c)
    far = j + side * (3 - 2 * j)
    return far + near * (1 - far // 2) * (1 - 2 * (far % 2))


def chip_at(c, k):
    side = c // 2
    near = c + side * (3 - 2 * c)
    far = k + near * (1 - k // 2) * (1 - 2 * (k % 2))
    return far + side * (3 - 2 * far)


def ffn_kernel(tok_hbm, cot_hbm, w_hbm, mask_ref, out_ref, ig_ref, x_out, h_out,
               x_buf, w_buf, keep, s1, r1, s2, r2, h_buf, o_own, pair_s, pair_r, z_s, z_r,
               local_sem, w_sem, send_sem, recv_sem,
               line_send, line_recv, col_recv):
    d = lax.axis_index("dp")
    r = lax.axis_index("row")
    c = lax.axis_index("col")
    tok_n = tok_hbm.shape[0]
    quarter = w_buf.shape[2]
    share = 4 * quarter
    half = x_buf.shape[2]
    feats = w_buf.shape[1]
    other = (1 - d, r, c)
    row_peer = {a: (d, flip(r, a), c) for a in (1, 2)}
    col_peer = {a: (d, r, (c + a) % 4) for a in (1, 2, 3)}

    tok_cp = pltpu.make_async_copy(tok_hbm, x_buf.at[0, d, pl.ds(0, tok_n)], local_sem.at[0])
    cot_cp = pltpu.make_async_copy(cot_hbm, x_buf.at[0, d, pl.ds(tok_n, tok_n)], local_sem.at[1])
    tok_cp.start()
    cot_cp.start()
    w_cps = []
    for t in (3, 1, 2, 0):
        q = flip(r, t)
        cols = pl.ds(pl.multiple_of(d * share + q * quarter, 128), quarter)
        cp = pltpu.make_async_copy(w_hbm.at[:, cols], w_buf.at[q], w_sem.at[t])
        cp.start()
        w_cps.append((q, cp))

    barrier = pltpu.get_barrier_semaphore()
    peers = [other] + list(row_peer.values()) + list(col_peer.values())
    for peer in peers:
        pl.semaphore_signal(barrier, inc=1, device_id=peer, device_id_type=pl.DeviceIdType.MESH)
    pl.semaphore_wait(barrier, len(peers))

    count = [0]
    msgs = {}

    def msg(name, src, dst, peer):
        i = count[0]
        count[0] += 1
        cp = pltpu.make_async_remote_copy(
            src_ref=src, dst_ref=dst, send_sem=send_sem.at[i], recv_sem=recv_sem.at[i],
            device_id=peer, device_id_type=pl.DeviceIdType.MESH)
        cp.start()
        msgs[name] = cp

    def arrive(name):
        msgs[name].wait_recv()

    tok_cp.wait()
    cot_cp.wait()
    lines = []

    def along(when, slot, step, chip, sem):
        cp = pltpu.make_async_remote_copy(
            src_ref=x_buf.at[slot, d], dst_ref=x_buf.at[place_of((c + 4 + step) % 4, chip), d],
            send_sem=line_send.at[sem], recv_sem=line_recv.at[place_of((c + 4 + step) % 4, chip)],
            device_id=(d, r, (c + 4 + step) % 4), device_id_type=pl.DeviceIdType.MESH)
        pl.when(when)(cp.start)
        lines.append((when, cp))

    along(c < 3, 0, 1, c, 0)
    along(c > 0, 0, -1, c, 1)
    msg(("xp", 0), x_buf.at[0, d], x_buf.at[0, d], other)

    for q, cp in w_cps:
        cp.wait()
        for i in range(feats // BLOCK):
            rows = pl.ds(i * BLOCK, BLOCK)
            w_buf[q, rows, :] = w_buf[q, rows, :] * mask_ref[q, pl.ds(i, 1), :].astype(jnp.bfloat16)

    def order(h):
        return (1, 2) if h == 0 else (2, 1)

    def part(h):
        return slice(h * quarter // 2, (h + 1) * quarter // 2)

    out_cps = []

    def fwd(s):
        pltpu.make_async_remote_copy(
            src_ref=x_buf.at[0, d], dst_ref=x_buf.at[s, d], send_sem=line_send.at[0],
            recv_sem=line_recv.at[s], device_id=other,
            device_id_type=pl.DeviceIdType.MESH).wait_recv()
        chip = chip_at(c, s)
        along((chip < c) & (c < 3), s, 1, chip, 2 * s)
        along((chip > c) & (c > 0), s, -1, chip, 2 * s + 1)
        msg(("xp", s), x_buf.at[s, d], x_buf.at[s, d], other)

    def stage_a(s):
        arrive(("xp", s))
        x = x_buf[s].reshape(2 * half, feats)
        cp = pltpu.make_async_copy(x_buf.at[s], x_out.at[s], local_sem.at[2 + s])
        cp.start()
        out_cps.append(cp)
        for k in (1, 0):
            for h in range(2):
                a = order(h)[0]
                q = flip(r, 3 if k else a)
                s1[s, h, k] = jnp.dot(x, w_buf[q, :, part(h)],
                                      preferred_element_type=jnp.float32).astype(s1.dtype)
                msg(("r1", s, h, k), s1.at[s, h, k], r1.at[s, h, k], row_peer[a])
        for k in (1, 0):
            for h in range(2):
                q = flip(r, order(h)[1] if k else 0)
                keep[s, h, k] = jnp.dot(x, w_buf[q, :, part(h)], preferred_element_type=jnp.float32)

    def stage_b(s):
        for h in range(2):
            b = order(h)[1]
            arrive(("r1", s, h, 1))
            s2[s, h] = (keep[s, h, 1] + r1[s, h, 1].astype(jnp.float32)).astype(s2.dtype)
            msg(("r2", s, h), s2.at[s, h], r2.at[s, h], row_peer[b])

    def stage_c(s):
        for h in range(2):
            a, b = order(h)
            arrive(("r1", s, h, 0))
            arrive(("r2", s, h))
            for p in range(2):
                lo = pl.ds(p * half, tok_n)
                hi = pl.ds(p * half + tok_n, tok_n)

                def total(rows):
                    return (keep[s, h, 0, rows, :] + r1[s, h, 0, rows, :].astype(jnp.float32)
                            + r2[s, h, rows, :].astype(jnp.float32))

                pre = total(lo)
                grad_hidden = total(hi)
                sig = jax.nn.sigmoid(pre)
                h_buf[s, r, h, lo, :] = (
                    grad_hidden * sig * (1.0 + pre * (1.0 - sig))).astype(jnp.bfloat16)
                h_buf[s, r, h, hi, :] = (pre * sig).astype(jnp.bfloat16)
            msg(("gb", s, h), h_buf.at[s, r, h], h_buf.at[s, r, h], row_peer[b])
            msg(("ga", s, h), h_buf.at[s, r, h], h_buf.at[s, r, h], row_peer[a])

    def stage_d(s):
        for h in range(2):
            a, b = order(h)
            arrive(("gb", s, h))
            q = flip(r, b)
            msg(("gf", s, h), h_buf.at[s, q, h], h_buf.at[s, q, h], row_peer[a])

    def stage_e(s):
        for h in range(2):
            arrive(("ga", s, h))
            arrive(("gf", s, h))
        cp = pltpu.make_async_copy(h_buf.at[s], h_out.at[:, :, pl.ds(s * 2 * half, 2 * half), :], local_sem.at[6 + s])
        cp.start()
        out_cps.append(cp)
        width = quarter

        def body(f, carry):
            rows = pl.ds(pl.multiple_of(f * width, width), width)
            acc = None
            for q in range(4):
                for h in range(2):
                    term = lax.dot_general(h_buf[s, q, h], w_buf[q, rows, part(h)],
                                           (((1,), (1,)), ((), ())),
                                           preferred_element_type=jnp.float32)
                    acc = term if acc is None else acc + term
            acc = acc.reshape(2, half, width)
            low, high = acc[0], acc[1]
            mine = jnp.where(d == 0, low, high)
            theirs = jnp.where(d == 0, high, low)
            o_own[s, :, rows] = mine
            pair_s[s, :, rows] = theirs.astype(pair_s.dtype)
            return carry

        lax.fori_loop(0, feats // width, body, 0)
        msg(("pp", s), pair_s.at[s], pair_r.at[s], other)

    def stage_f(s):
        arrive(("pp", s))
        if s == 0:
            o_own[s] = o_own[s] + pair_r[s].astype(jnp.float32)
        else:
            z_s[s] = (o_own[s] + pair_r[s].astype(jnp.float32)).astype(z_s.dtype)
            chip = chip_at(c, s)
            slot = place_of(chip, c)
            i = count[0]
            count[0] += 1
            cp = pltpu.make_async_remote_copy(
                src_ref=z_s.at[s], dst_ref=z_r.at[slot], send_sem=send_sem.at[i],
                recv_sem=col_recv.at[slot], device_id=(d, r, chip),
                device_id_type=pl.DeviceIdType.MESH)
            cp.start()
            msgs[("zz", s)] = cp

    stage_a(0)
    fwd(1)
    stage_b(0)
    stage_a(1)
    fwd(2)
    stage_c(0)
    stage_b(1)
    stage_d(0)
    stage_a(2)
    stage_c(1)
    fwd(3)
    stage_b(2)
    stage_d(1)
    stage_a(3)
    stage_c(2)
    stage_b(3)
    stage_e(0)
    stage_d(2)
    stage_c(3)
    stage_e(1)
    stage_d(3)
    stage_f(0)
    stage_f(1)
    stage_e(2)
    stage_f(2)
    stage_e(3)
    stage_f(3)

    total = o_own[0]
    for s in (1, 2, 3):
        pltpu.make_async_remote_copy(
            src_ref=z_s.at[s], dst_ref=z_r.at[s], send_sem=send_sem.at[0],
            recv_sem=col_recv.at[s], device_id=other,
            device_id_type=pl.DeviceIdType.MESH).wait_recv()
        total = total + z_r[s].astype(jnp.float32)
    base = x_buf[0, d].astype(jnp.float32)
    out_ref[...] = (base[:tok_n] + total[tok_n:]).astype(jnp.bfloat16)
    ig_ref[...] = (base[tok_n:] + total[:tok_n]).astype(jnp.bfloat16)
    for cp in out_cps:
        cp.wait()
    for cp in msgs.values():
        cp.wait_send()
    for when, cp in lines:
        pl.when(when)(cp.wait_send)


def grad_kernel(scale, mask_ref, x_ref, h_ref, out_ref):
    i = pl.program_id(0)
    rows = x_ref.shape[1]
    blocks = h_ref.shape[0] * h_ref.shape[2] // BLOCK
    per = h_ref.shape[2] // BLOCK
    lanes = 128
    step = blocks * BLOCK // lanes
    out_ref[...] = jnp.zeros_like(out_ref)
    for j in range(blocks):
        def put(value):
            for k in range(BLOCK // lanes):
                place = j * (BLOCK // lanes) + k
                out_ref[pl.ds(place, rows, stride=step), :] = value[:, k * lanes:(k + 1) * lanes]

        @pl.when(mask_ref[i, j] != 0)
        def _():
            h = h_ref[j // per, :, (j % per) * BLOCK:(j % per + 1) * BLOCK]
            put(lax.dot_general(x_ref[...], h, (((0,), (0,)), ((), ())),
                                preferred_element_type=jnp.float32) * scale)


def fast_on_device(tokens, cotangent, weight, block_mask):
    tok_n, feats = tokens.shape
    share = weight.shape[1] // lax.axis_size("dp")
    quarter = share // 4
    half = 2 * tok_n
    d = lax.axis_index("dp")
    tok_total = tok_n * lax.axis_size("col") * lax.axis_size("dp")
    share_mask = lax.dynamic_slice_in_dim(block_mask, d * (share // BLOCK), share // BLOCK, 1)
    wide = jnp.repeat(share_mask.astype(jnp.float32), BLOCK, axis=1)
    wide = wide.reshape(feats // BLOCK, 4, quarter).transpose(1, 0, 2)
    bf, f32 = jnp.bfloat16, jnp.float32
    vmem = pl.BlockSpec(memory_space=pltpu.VMEM)
    hbm = pl.BlockSpec(memory_space=pl.ANY)
    n_msg = 59
    piece = quarter // 2
    out, ig, x_all, h_all = pl.pallas_call(
        ffn_kernel,
        out_shape=(
            jax.ShapeDtypeStruct((tok_n, feats), bf),
            jax.ShapeDtypeStruct((tok_n, feats), bf),
            jax.ShapeDtypeStruct((4, 2, half, feats), bf),
            jax.ShapeDtypeStruct((4, 2, 8 * half, quarter // 2), bf),
        ),
        in_specs=[hbm, hbm, hbm, vmem],
        out_specs=(vmem, vmem, hbm, hbm),
        scratch_shapes=[
            pltpu.VMEM((4, 2, half, feats), bf),
            pltpu.VMEM((4, feats, quarter), bf),
            pltpu.VMEM((4, 2, 2, 2 * half, piece), f32),
            pltpu.VMEM((4, 2, 2, 2 * half, piece), RS1_TYPE),
            pltpu.VMEM((4, 2, 2, 2 * half, piece), RS1_TYPE),
            pltpu.VMEM((4, 2, 2 * half, piece), RS2_TYPE),
            pltpu.VMEM((4, 2, 2 * half, piece), RS2_TYPE),
            pltpu.VMEM((4, 4, 2, 2 * half, piece), bf),
            pltpu.VMEM((4, half, feats), f32),
            pltpu.VMEM((4, half, feats), PAIR_TYPE),
            pltpu.VMEM((4, half, feats), PAIR_TYPE),
            pltpu.VMEM((4, half, feats), COL_TYPE),
            pltpu.VMEM((4, half, feats), COL_TYPE),
            pltpu.SemaphoreType.DMA((10,)),
            pltpu.SemaphoreType.DMA((4,)),
            pltpu.SemaphoreType.DMA((n_msg,)),
            pltpu.SemaphoreType.DMA((n_msg,)),
            pltpu.SemaphoreType.DMA((8,)),
            pltpu.SemaphoreType.DMA((4,)),
            pltpu.SemaphoreType.DMA((4,)),
        ],
        compiler_params=pltpu.CompilerParams(
            collective_id=0, has_side_effects=True, vmem_limit_bytes=60000 * 1024),
    )(tokens, cotangent, weight, wide)
    x_all = x_all.reshape(8 * half, feats)
    h_all = h_all.reshape(8, 8 * half, piece)
    lines = share // 128
    flat = pl.pallas_call(
        functools.partial(grad_kernel, 1.0 / math.sqrt(tok_total)),
        grid_spec=pltpu.PrefetchScalarGridSpec(
            num_scalar_prefetch=1,
            grid=(feats // BLOCK,),
            in_specs=[
                pl.BlockSpec((8 * half, BLOCK), lambda i, m: (0, i)),
                pl.BlockSpec((8, 8 * half, piece), lambda i, m: (0, 0, 0)),
            ],
            out_specs=pl.BlockSpec((BLOCK * lines, 128), lambda i, m: (i, 0)),
        ),
        out_shape=jax.ShapeDtypeStruct((feats * lines, 128), f32),
    )(share_mask, x_all, h_all)
    return out, ig, flat.reshape(feats, 1, share)


def partner(block, axis, stride):
    count = lax.axis_size(axis)
    route = []
    for low in range(count):
        high = low | 1 << stride
        if high != low and high < count:
            route += [(low, high), (high, low)]
    return lax.ppermute(block, axis, route)


def expand_mask(block_mask):
    kept_blocks = block_mask.astype(jnp.bfloat16)
    return jnp.repeat(jnp.repeat(kept_blocks, BLOCK, axis=0), BLOCK, axis=1)


def slope_times(grad_hidden, pre):
    sigmoid_pre = jax.nn.sigmoid(pre)
    return (grad_hidden * sigmoid_pre * (1.0 + pre * (1.0 - sigmoid_pre))).astype(jnp.bfloat16)


def times_transpose(left, masked):
    return lax.dot_general(
        left, masked, (((1,), (1,)), ((), ())), preferred_element_type=jnp.float32
    )


def on_device(tokens, cotangent, weight, block_mask):
    kept = expand_mask(block_mask)
    masked = weight * kept
    tok_count = tokens.shape[0]
    tok_rows, cot_rows = (
        lax.all_gather(tokens, "col", axis=0, tiled=True),
        lax.all_gather(cotangent, "col", axis=0, tiled=True),
    )
    pre_part = jnp.dot(tok_rows, masked, preferred_element_type=jnp.float32)
    pre = lax.psum(pre_part, "row")
    hidden = jax.nn.silu(pre).astype(jnp.bfloat16)
    grad_part = jnp.dot(cot_rows, masked, preferred_element_type=jnp.float32)
    grad_hidden = lax.psum(grad_part, "row")
    grad_pre = slope_times(grad_hidden, pre)
    projected = lax.psum_scatter(
        times_transpose(hidden, masked), "col", scatter_dimension=0, tiled=True
    )
    output = (tokens.astype(jnp.float32) + projected).astype(jnp.bfloat16)
    back = lax.psum_scatter(
        times_transpose(grad_pre, masked), "col", scatter_dimension=0, tiled=True
    )
    input_grad = (cotangent.astype(jnp.float32) + back).astype(jnp.bfloat16)
    tok_total = tok_count * lax.axis_size("col") * lax.axis_size("dp")
    norm_scale = 1.0 / math.sqrt(tok_total)
    feat_rows = masked.shape[0]
    share_cols = masked.shape[1] // lax.axis_size("dp")
    dp_index = lax.axis_index("dp")
    low_bit = dp_index % 2
    groups = lax.axis_size("dp") // 2
    row_total = hidden.shape[0]
    hid_split = hidden.reshape(row_total, groups, 2, share_cols)
    grad_split = grad_pre.reshape(row_total, groups, 2, share_cols)
    hid_class = lax.dynamic_index_in_dim(hid_split, low_bit, 2, keepdims=False)
    grad_class = lax.dynamic_index_in_dim(grad_split, low_bit, 2, keepdims=False)
    hid_other = lax.dynamic_index_in_dim(hid_split, 1 - low_bit, 2, keepdims=False)
    grad_other = lax.dynamic_index_in_dim(grad_split, 1 - low_bit, 2, keepdims=False)
    other_tok, other_cot, other_hid, other_grad = partner(
        (tok_rows, cot_rows, hid_other, grad_other), "dp", 0
    )
    pair_tok = jnp.concatenate([tok_rows, other_tok], axis=0)
    pair_cot = jnp.concatenate([cot_rows, other_cot], axis=0)
    pair_hid = jnp.concatenate([hid_class, other_hid], axis=0)
    pair_grad = jnp.concatenate([grad_class, other_grad], axis=0)
    partial_value = jnp.einsum(
        "td,tqj->qdj", pair_cot, pair_hid, preferred_element_type=jnp.float32
    )
    partial_value = partial_value + jnp.einsum(
        "td,tqj->qdj", pair_tok, pair_grad, preferred_element_type=jnp.float32
    )
    bit_count = lax.axis_size("dp").bit_length() - 1
    for bit_level in range(bit_count - 1, 0, -1):
        halves = partial_value.reshape(2, partial_value.shape[0] // 2, feat_rows, share_cols)
        my_half = dp_index // 2**bit_level % 2
        keep_part = lax.dynamic_index_in_dim(halves, my_half, 0, keepdims=False)
        send_part = lax.dynamic_index_in_dim(halves, 1 - my_half, 0, keepdims=False)
        partial_value = keep_part + partner(send_part, "dp", bit_level)
    kept_share = lax.dynamic_slice_in_dim(kept, dp_index * share_cols, share_cols, 1)
    summed = partial_value[0] * kept_share.astype(jnp.float32) * norm_scale
    weight_grad = summed.reshape(feat_rows, 1, share_cols)
    return (output, input_grad, weight_grad)


def solution(mesh):
    in_specs = (P(("dp", "col"), "row"), P(("dp", "col"), "row"), P("row", "col"), P("row", "col"))
    out_specs = (P(("dp", "col"), "row"), P(("dp", "col"), "row"), P("row", "dp", "col"))
    sizes = (mesh.shape["dp"], mesh.shape["row"], mesh.shape["col"])
    body = fast_on_device if sizes == (2, 4, 4) else on_device
    return jax.shard_map(
        body, mesh=mesh, in_specs=in_specs, out_specs=out_specs, check_vma=False
    )
```

```python
import functools
import math

import jax
import jax.numpy as jnp
from jax import lax
from jax.experimental import pallas as pl
from jax.experimental.pallas import tpu as pltpu
from jax.sharding import PartitionSpec as P

BLOCK = 256
RS1_TYPE = jnp.bfloat16
RS2_TYPE = jnp.bfloat16
PAIR_TYPE = jnp.float32
COL_TYPE = jnp.bfloat16


def flip1(i):
    return i + 1 - 2 * (i % 2)


def flip2(i):
    return (i + 2) % 4


def flip(i, bits):
    if bits == 0:
        return i
    if bits == 1:
        return flip1(i)
    if bits == 2:
        return flip2(i)
    return 3 - i


def place_of(c, j):
    side = c // 2
    near = c + side * (3 - 2 * c)
    far = j + side * (3 - 2 * j)
    return far + near * (1 - far // 2) * (1 - 2 * (far % 2))


def chip_at(c, k):
    side = c // 2
    near = c + side * (3 - 2 * c)
    far = k + near * (1 - k // 2) * (1 - 2 * (k % 2))
    return far + side * (3 - 2 * far)


def ffn_kernel(tok_hbm, cot_hbm, w_hbm, mask_ref, out_ref, ig_ref, x_out, h_out,
               x_buf, w_buf, keep, s1, r1, s2, r2, h_buf, o_own, pair_s, pair_r, z_s, z_r,
               local_sem, w_sem, send_sem, recv_sem,
               line_send, line_recv, col_recv):
    d = lax.axis_index("dp")
    r = lax.axis_index("row")
    c = lax.axis_index("col")
    tok_n = tok_hbm.shape[0]
    quarter = w_buf.shape[2]
    share = 4 * quarter
    half = x_buf.shape[2]
    feats = w_buf.shape[1]
    other = (1 - d, r, c)
    row_peer = {a: (d, flip(r, a), c) for a in (1, 2)}
    col_peer = {a: (d, r, (c + a) % 4) for a in (1, 2, 3)}

    tok_cp = pltpu.make_async_copy(tok_hbm, x_buf.at[0, d, pl.ds(0, tok_n)], local_sem.at[0])
    cot_cp = pltpu.make_async_copy(cot_hbm, x_buf.at[0, d, pl.ds(tok_n, tok_n)], local_sem.at[1])
    tok_cp.start()
    cot_cp.start()
    w_cps = []
    for t in (3, 1, 2, 0):
        q = flip(r, t)
        cols = pl.ds(pl.multiple_of(d * share + q * quarter, 128), quarter)
        cp = pltpu.make_async_copy(w_hbm.at[:, cols], w_buf.at[q], w_sem.at[t])
        cp.start()
        w_cps.append((q, cp))

    barrier = pltpu.get_barrier_semaphore()
    peers = [other] + list(row_peer.values()) + list(col_peer.values())
    for peer in peers:
        pl.semaphore_signal(barrier, inc=1, device_id=peer, device_id_type=pl.DeviceIdType.MESH)
    pl.semaphore_wait(barrier, len(peers))

    count = [0]
    msgs = {}

    def msg(name, src, dst, peer):
        i = count[0]
        count[0] += 1
        cp = pltpu.make_async_remote_copy(
            src_ref=src, dst_ref=dst, send_sem=send_sem.at[i], recv_sem=recv_sem.at[i],
            device_id=peer, device_id_type=pl.DeviceIdType.MESH)
        cp.start()
        msgs[name] = cp

    def arrive(name):
        msgs[name].wait_recv()

    tok_cp.wait()
    cot_cp.wait()
    lines = []

    def along(when, slot, step, chip, sem):
        cp = pltpu.make_async_remote_copy(
            src_ref=x_buf.at[slot, d], dst_ref=x_buf.at[place_of((c + 4 + step) % 4, chip), d],
            send_sem=line_send.at[sem], recv_sem=line_recv.at[place_of((c + 4 + step) % 4, chip)],
            device_id=(d, r, (c + 4 + step) % 4), device_id_type=pl.DeviceIdType.MESH)
        pl.when(when)(cp.start)
        lines.append((when, cp))

    along(c < 3, 0, 1, c, 0)
    along(c > 0, 0, -1, c, 1)
    msg(("xp", 0), x_buf.at[0, d], x_buf.at[0, d], other)

    for q, cp in w_cps:
        cp.wait()
        for i in range(feats // BLOCK):
            rows = pl.ds(i * BLOCK, BLOCK)
            w_buf[q, rows, :] = w_buf[q, rows, :] * mask_ref[q, pl.ds(i, 1), :].astype(jnp.bfloat16)

    def order(h):
        return (1, 2) if h == 0 else (2, 1)

    def part(h):
        return slice(h * quarter // 2, (h + 1) * quarter // 2)

    out_cps = []

    def fwd(s):
        pltpu.make_async_remote_copy(
            src_ref=x_buf.at[0, d], dst_ref=x_buf.at[s, d], send_sem=line_send.at[0],
            recv_sem=line_recv.at[s], device_id=other,
            device_id_type=pl.DeviceIdType.MESH).wait_recv()
        chip = chip_at(c, s)
        along((chip < c) & (c < 3), s, 1, chip, 2 * s)
        along((chip > c) & (c > 0), s, -1, chip, 2 * s + 1)
        msg(("xp", s), x_buf.at[s, d], x_buf.at[s, d], other)

    def stage_a(s):
        arrive(("xp", s))
        x = x_buf[s].reshape(2 * half, feats)
        cp = pltpu.make_async_copy(x_buf.at[s], x_out.at[s], local_sem.at[2 + s])
        cp.start()
        out_cps.append(cp)
        for k in (1, 0):
            for h in range(2):
                a = order(h)[0]
                q = flip(r, 3 if k else a)
                s1[s, h, k] = jnp.dot(x, w_buf[q, :, part(h)],
                                      preferred_element_type=jnp.float32).astype(s1.dtype)
                msg(("r1", s, h, k), s1.at[s, h, k], r1.at[s, h, k], row_peer[a])
        for k in (1, 0):
            for h in range(2):
                q = flip(r, order(h)[1] if k else 0)
                keep[s, h, k] = jnp.dot(x, w_buf[q, :, part(h)], preferred_element_type=jnp.float32)

    def stage_b(s):
        for h in range(2):
            b = order(h)[1]
            arrive(("r1", s, h, 1))
            s2[s, h] = (keep[s, h, 1] + r1[s, h, 1].astype(jnp.float32)).astype(s2.dtype)
            msg(("r2", s, h), s2.at[s, h], r2.at[s, h], row_peer[b])

    def stage_c(s):
        for h in range(2):
            a, b = order(h)
            arrive(("r1", s, h, 0))
            arrive(("r2", s, h))
            for p in range(2):
                lo = pl.ds(p * half, tok_n)
                hi = pl.ds(p * half + tok_n, tok_n)

                def total(rows):
                    return (keep[s, h, 0, rows, :] + r1[s, h, 0, rows, :].astype(jnp.float32)
                            + r2[s, h, rows, :].astype(jnp.float32))

                pre = total(lo)
                grad_hidden = total(hi)
                sig = jax.nn.sigmoid(pre)
                h_buf[s, r, h, lo, :] = (
                    grad_hidden * sig * (1.0 + pre * (1.0 - sig))).astype(jnp.bfloat16)
                h_buf[s, r, h, hi, :] = (pre * sig).astype(jnp.bfloat16)
            msg(("gb", s, h), h_buf.at[s, r, h], h_buf.at[s, r, h], row_peer[b])
            msg(("ga", s, h), h_buf.at[s, r, h], h_buf.at[s, r, h], row_peer[a])

    def stage_d(s):
        for h in range(2):
            a, b = order(h)
            arrive(("gb", s, h))
            q = flip(r, b)
            msg(("gf", s, h), h_buf.at[s, q, h], h_buf.at[s, q, h], row_peer[a])

    def stage_e(s):
        for h in range(2):
            arrive(("ga", s, h))
            arrive(("gf", s, h))
        cp = pltpu.make_async_copy(h_buf.at[s], h_out.at[:, :, pl.ds(s * 2 * half, 2 * half), :], local_sem.at[6 + s])
        cp.start()
        out_cps.append(cp)
        width = quarter

        def body(f, carry):
            rows = pl.ds(pl.multiple_of(f * width, width), width)
            acc = None
            for q in range(4):
                for h in range(2):
                    term = lax.dot_general(h_buf[s, q, h], w_buf[q, rows, part(h)],
                                           (((1,), (1,)), ((), ())),
                                           preferred_element_type=jnp.float32)
                    acc = term if acc is None else acc + term
            acc = acc.reshape(2, half, width)
            low, high = acc[0], acc[1]
            mine = jnp.where(d == 0, low, high)
            theirs = jnp.where(d == 0, high, low)
            o_own[s, :, rows] = mine
            pair_s[s, :, rows] = theirs.astype(pair_s.dtype)
            return carry

        tiles = feats // width
        for u in range(2):
            lax.fori_loop(u * tiles // 2, (u + 1) * tiles // 2, body, 0)
            msg(("pp", s, u), pair_s.at[s, :, side(u)], pair_r.at[s, :, side(u)], other)

    def side(u):
        return pl.ds(u * feats // 2, feats // 2)

    def stage_f(s):
        for u in range(2):
            arrive(("pp", s, u))
            summed = o_own[s, :, side(u)] + pair_r[s, :, side(u)].astype(jnp.float32)
            if s == 0:
                o_own[s, :, side(u)] = summed
                continue
            z_s[s, :, side(u)] = summed.astype(z_s.dtype)
            chip = chip_at(c, s)
            slot = place_of(chip, c)
            i = count[0]
            count[0] += 1
            cp = pltpu.make_async_remote_copy(
                src_ref=z_s.at[s, :, side(u)], dst_ref=z_r.at[slot, :, side(u)],
                send_sem=send_sem.at[i], recv_sem=col_recv.at[slot, u], device_id=(d, r, chip),
                device_id_type=pl.DeviceIdType.MESH)
            cp.start()
            msgs[("zz", s, u)] = cp

    stage_a(0)
    fwd(1)
    stage_b(0)
    stage_a(1)
    fwd(2)
    stage_c(0)
    stage_b(1)
    stage_d(0)
    stage_a(2)
    stage_c(1)
    fwd(3)
    stage_b(2)
    stage_d(1)
    stage_a(3)
    stage_c(2)
    stage_b(3)
    stage_e(0)
    stage_d(2)
    stage_c(3)
    stage_e(1)
    stage_d(3)
    stage_f(0)
    stage_f(1)
    stage_e(2)
    stage_f(2)
    stage_e(3)
    stage_f(3)

    for u in range(2):
        total = o_own[0, :, side(u)]
        for s in (1, 2, 3):
            pltpu.make_async_remote_copy(
                src_ref=z_s.at[s, :, side(u)], dst_ref=z_r.at[s, :, side(u)],
                send_sem=send_sem.at[0], recv_sem=col_recv.at[s, u], device_id=other,
                device_id_type=pl.DeviceIdType.MESH).wait_recv()
            total = total + z_r[s, :, side(u)].astype(jnp.float32)
        base = x_buf[0, d, :, side(u)].astype(jnp.float32)
        out_ref[:, side(u)] = (base[:tok_n] + total[tok_n:]).astype(jnp.bfloat16)
        ig_ref[:, side(u)] = (base[tok_n:] + total[:tok_n]).astype(jnp.bfloat16)
    for cp in out_cps:
        cp.wait()
    for cp in msgs.values():
        cp.wait_send()
    for when, cp in lines:
        pl.when(when)(cp.wait_send)


def grad_kernel(scale, mask_ref, x_ref, h_ref, y_ref, g_ref, out_ref, y_out, g_out):
    i = pl.program_id(0)

    @pl.when(i == 0)
    def _():
        y_out[...] = y_ref[...]
        g_out[...] = g_ref[...]

    rows = x_ref.shape[1]
    blocks = h_ref.shape[0] * h_ref.shape[2] // BLOCK
    per = h_ref.shape[2] // BLOCK
    lanes = 128
    step = blocks * BLOCK // lanes
    out_ref[...] = jnp.zeros_like(out_ref)
    for j in range(blocks):
        def put(value):
            for k in range(BLOCK // lanes):
                place = j * (BLOCK // lanes) + k
                out_ref[pl.ds(place, rows, stride=step), :] = value[:, k * lanes:(k + 1) * lanes]

        @pl.when(mask_ref[i, j] != 0)
        def _():
            h = h_ref[j // per, :, (j % per) * BLOCK:(j % per + 1) * BLOCK]
            put(lax.dot_general(x_ref[...], h, (((0,), (0,)), ((), ())),
                                preferred_element_type=jnp.float32) * scale)


def fast_on_device(tokens, cotangent, weight, block_mask):
    tok_n, feats = tokens.shape
    share = weight.shape[1] // lax.axis_size("dp")
    quarter = share // 4
    half = 2 * tok_n
    d = lax.axis_index("dp")
    tok_total = tok_n * lax.axis_size("col") * lax.axis_size("dp")
    share_mask = lax.dynamic_slice_in_dim(block_mask, d * (share // BLOCK), share // BLOCK, 1)
    wide = jnp.repeat(share_mask.astype(jnp.float32), BLOCK, axis=1)
    wide = wide.reshape(feats // BLOCK, 4, quarter).transpose(1, 0, 2)
    bf, f32 = jnp.bfloat16, jnp.float32
    vmem = pl.BlockSpec(memory_space=pltpu.VMEM)
    hbm = pl.BlockSpec(memory_space=pl.ANY)
    n_msg = 66
    piece = quarter // 2
    out, ig, x_all, h_all = pl.pallas_call(
        ffn_kernel,
        out_shape=(
            jax.ShapeDtypeStruct((tok_n, feats), bf),
            jax.ShapeDtypeStruct((tok_n, feats), bf),
            jax.ShapeDtypeStruct((4, 2, half, feats), bf),
            jax.ShapeDtypeStruct((4, 2, 8 * half, quarter // 2), bf),
        ),
        in_specs=[hbm, hbm, hbm, vmem],
        out_specs=(vmem, vmem, hbm, hbm),
        scratch_shapes=[
            pltpu.VMEM((4, 2, half, feats), bf),
            pltpu.VMEM((4, feats, quarter), bf),
            pltpu.VMEM((4, 2, 2, 2 * half, piece), f32),
            pltpu.VMEM((4, 2, 2, 2 * half, piece), RS1_TYPE),
            pltpu.VMEM((4, 2, 2, 2 * half, piece), RS1_TYPE),
            pltpu.VMEM((4, 2, 2 * half, piece), RS2_TYPE),
            pltpu.VMEM((4, 2, 2 * half, piece), RS2_TYPE),
            pltpu.VMEM((4, 4, 2, 2 * half, piece), bf),
            pltpu.VMEM((4, half, feats), f32),
            pltpu.VMEM((4, half, feats), PAIR_TYPE),
            pltpu.VMEM((4, half, feats), PAIR_TYPE),
            pltpu.VMEM((4, half, feats), COL_TYPE),
            pltpu.VMEM((4, half, feats), COL_TYPE),
            pltpu.SemaphoreType.DMA((10,)),
            pltpu.SemaphoreType.DMA((4,)),
            pltpu.SemaphoreType.DMA((n_msg,)),
            pltpu.SemaphoreType.DMA((n_msg,)),
            pltpu.SemaphoreType.DMA((8,)),
            pltpu.SemaphoreType.DMA((4,)),
            pltpu.SemaphoreType.DMA((4, 2)),
        ],
        compiler_params=pltpu.CompilerParams(
            collective_id=0, has_side_effects=True, vmem_limit_bytes=60000 * 1024),
    )(tokens, cotangent, weight, wide)
    x_all = x_all.reshape(8 * half, feats)
    h_all = h_all.reshape(8, 8 * half, piece)
    lines = share // 128
    whole = pl.BlockSpec((tok_n, feats), lambda i, m: (0, 0))
    flat, out, ig = pl.pallas_call(
        functools.partial(grad_kernel, 1.0 / math.sqrt(tok_total)),
        grid_spec=pltpu.PrefetchScalarGridSpec(
            num_scalar_prefetch=1,
            grid=(feats // BLOCK,),
            in_specs=[
                pl.BlockSpec((8 * half, BLOCK), lambda i, m: (0, i)),
                pl.BlockSpec((8, 8 * half, piece), lambda i, m: (0, 0, 0)),
                whole,
                whole,
            ],
            out_specs=(
                pl.BlockSpec((BLOCK * lines, 128), lambda i, m: (i, 0)),
                whole,
                whole,
            ),
        ),
        out_shape=(
            jax.ShapeDtypeStruct((feats * lines, 128), f32),
            jax.ShapeDtypeStruct((tok_n, feats), bf),
            jax.ShapeDtypeStruct((tok_n, feats), bf),
        ),
    )(share_mask, x_all, h_all, out, ig)
    return out, ig, flat.reshape(feats, 1, share)


def partner(block, axis, stride):
    count = lax.axis_size(axis)
    route = []
    for low in range(count):
        high = low | 1 << stride
        if high != low and high < count:
            route += [(low, high), (high, low)]
    return lax.ppermute(block, axis, route)


def expand_mask(block_mask):
    kept_blocks = block_mask.astype(jnp.bfloat16)
    return jnp.repeat(jnp.repeat(kept_blocks, BLOCK, axis=0), BLOCK, axis=1)


def slope_times(grad_hidden, pre):
    sigmoid_pre = jax.nn.sigmoid(pre)
    return (grad_hidden * sigmoid_pre * (1.0 + pre * (1.0 - sigmoid_pre))).astype(jnp.bfloat16)


def times_transpose(left, masked):
    return lax.dot_general(
        left, masked, (((1,), (1,)), ((), ())), preferred_element_type=jnp.float32
    )


def on_device(tokens, cotangent, weight, block_mask):
    kept = expand_mask(block_mask)
    masked = weight * kept
    tok_count = tokens.shape[0]
    tok_rows, cot_rows = (
        lax.all_gather(tokens, "col", axis=0, tiled=True),
        lax.all_gather(cotangent, "col", axis=0, tiled=True),
    )
    pre_part = jnp.dot(tok_rows, masked, preferred_element_type=jnp.float32)
    pre = lax.psum(pre_part, "row")
    hidden = jax.nn.silu(pre).astype(jnp.bfloat16)
    grad_part = jnp.dot(cot_rows, masked, preferred_element_type=jnp.float32)
    grad_hidden = lax.psum(grad_part, "row")
    grad_pre = slope_times(grad_hidden, pre)
    projected = lax.psum_scatter(
        times_transpose(hidden, masked), "col", scatter_dimension=0, tiled=True
    )
    output = (tokens.astype(jnp.float32) + projected).astype(jnp.bfloat16)
    back = lax.psum_scatter(
        times_transpose(grad_pre, masked), "col", scatter_dimension=0, tiled=True
    )
    input_grad = (cotangent.astype(jnp.float32) + back).astype(jnp.bfloat16)
    tok_total = tok_count * lax.axis_size("col") * lax.axis_size("dp")
    norm_scale = 1.0 / math.sqrt(tok_total)
    feat_rows = masked.shape[0]
    share_cols = masked.shape[1] // lax.axis_size("dp")
    dp_index = lax.axis_index("dp")
    low_bit = dp_index % 2
    groups = lax.axis_size("dp") // 2
    row_total = hidden.shape[0]
    hid_split = hidden.reshape(row_total, groups, 2, share_cols)
    grad_split = grad_pre.reshape(row_total, groups, 2, share_cols)
    hid_class = lax.dynamic_index_in_dim(hid_split, low_bit, 2, keepdims=False)
    grad_class = lax.dynamic_index_in_dim(grad_split, low_bit, 2, keepdims=False)
    hid_other = lax.dynamic_index_in_dim(hid_split, 1 - low_bit, 2, keepdims=False)
    grad_other = lax.dynamic_index_in_dim(grad_split, 1 - low_bit, 2, keepdims=False)
    other_tok, other_cot, other_hid, other_grad = partner(
        (tok_rows, cot_rows, hid_other, grad_other), "dp", 0
    )
    pair_tok = jnp.concatenate([tok_rows, other_tok], axis=0)
    pair_cot = jnp.concatenate([cot_rows, other_cot], axis=0)
    pair_hid = jnp.concatenate([hid_class, other_hid], axis=0)
    pair_grad = jnp.concatenate([grad_class, other_grad], axis=0)
    partial_value = jnp.einsum(
        "td,tqj->qdj", pair_cot, pair_hid, preferred_element_type=jnp.float32
    )
    partial_value = partial_value + jnp.einsum(
        "td,tqj->qdj", pair_tok, pair_grad, preferred_element_type=jnp.float32
    )
    bit_count = lax.axis_size("dp").bit_length() - 1
    for bit_level in range(bit_count - 1, 0, -1):
        halves = partial_value.reshape(2, partial_value.shape[0] // 2, feat_rows, share_cols)
        my_half = dp_index // 2**bit_level % 2
        keep_part = lax.dynamic_index_in_dim(halves, my_half, 0, keepdims=False)
        send_part = lax.dynamic_index_in_dim(halves, 1 - my_half, 0, keepdims=False)
        partial_value = keep_part + partner(send_part, "dp", bit_level)
    kept_share = lax.dynamic_slice_in_dim(kept, dp_index * share_cols, share_cols, 1)
    summed = partial_value[0] * kept_share.astype(jnp.float32) * norm_scale
    weight_grad = summed.reshape(feat_rows, 1, share_cols)
    return (output, input_grad, weight_grad)


def solution(mesh):
    in_specs = (P(("dp", "col"), "row"), P(("dp", "col"), "row"), P("row", "col"), P("row", "col"))
    out_specs = (P(("dp", "col"), "row"), P(("dp", "col"), "row"), P("row", "dp", "col"))
    sizes = (mesh.shape["dp"], mesh.shape["row"], mesh.shape["col"])
    body = fast_on_device if sizes == (2, 4, 4) else on_device
    return jax.shard_map(
        body, mesh=mesh, in_specs=in_specs, out_specs=out_specs, check_vma=False
    )
```
